32 devices in a mesh: row: 8 (over z, x), col: 4 (over y, core).
Axes of the slice: x: 2, y: 2, z: 4, core: 2. Of those that a mesh axis runs over, the one named last changes fastest.
Arguments:
- blocks: bfloat16 [8, 4, 256, 128, 128], P('row', 'col'), may hold values from -0.25 to 0.25
- block_rows: int32 [8, 4, 256], P('row', 'col'), may hold values from 0 to 255
- block_cols: int32 [8, 4, 256], P('row', 'col'), may hold values from 0 to 255
- counts: int32 [8, 4], P('row', 'col'), may hold values from 85 to 256, as said below
- data: float32 [262144], P('row'), may hold values from -16 to 16
Outputs:
- solution: float32 [131072], P('col')
- search: float32 [131072], P('col')
- data_basis: float32 [262144], P('row')
The draws below stay inside these ranges and needn't reach their ends.
Inputs may be any that keep to these rules, and one draw needn't show every extreme that they name: `counts`: every tile has between 85 and 256 live slots; some tile has exactly 256.
All inputs are finite; a program needn't handle non-finite values.
Results may differ from the reference program's by a relative error of at most 0.013.
Values sent between devices are 32-bit elements; how exact they have to be, the bound alone decides.
No kernel may reach another device: no remote copies, remote signals or barrier semaphores. Data moves between devices by JAX's collectives and lax.ppermute only.
A program may use at most 64 MiB of HBM per device.

```python
import jax
import jax.numpy as jnp
from jax import lax

BLOCK = 128
TILE_ROWS = 256
TILE_COLS = 256
SLOTS = 256
ITERS = 3
DATA_LEN = 262144
N_ROW = 8
N_COL = 4


def draw_counts(key, part):
    first, second = jax.random.split(key)
    values = jax.random.randint(first, (N_ROW * N_COL,), SLOTS // 3, SLOTS + 1)
    chosen = jax.random.randint(second, (), 0, N_ROW * N_COL)
    values = jnp.where(jnp.arange(N_ROW * N_COL) == chosen, SLOTS, values)
    return values.reshape(N_ROW, N_COL).astype(jnp.int32)


def draw_data(key, part):
    ramp = 1.0 + 2.0 * jnp.arange(DATA_LEN, dtype=jnp.float32) / (DATA_LEN - 1)
    values = jnp.clip(jax.random.normal(key, (DATA_LEN,), jnp.float32), -5.3, 5.3) * ramp
    return values.astype(jnp.float32)


def set_ends(values, own_key, smallest, largest):
    longest = values.shape.index(max(values.shape))
    spots = []
    for shift in (0, 1):
        where = [jax.random.randint(jax.random.fold_in(own_key, axis), (), 0, length) for axis, length in enumerate(values.shape)]
        where[longest] = (where[longest] + shift) % values.shape[longest]
        spots.append(tuple(where))
    return values.at[spots[0]].set(smallest).at[spots[1]].set(largest)


def steps_of(key, dims, cuts, low, top_value):
    def one(axis_at, blocks):
        draws = jax.random.uniform(jax.random.fold_in(jax.random.fold_in(key, 6), axis_at), (blocks,), jnp.float32, low / len(cuts), top_value / len(cuts))
        return jnp.repeat(jnp.exp(draws), dims[axis_at] // blocks).reshape((-1,) + (1,) * (len(dims) - axis_at - 1))

    level = one(*cuts[0])
    for cut in cuts[1:]:
        level = level * one(*cut)
    return level


def scatter_about(stream_key, shape, width, reach, pieces=(), kind=jnp.bfloat16):
    loudness = steps_of(stream_key, shape, pieces, -0.22, 0.18) if pieces else 1.0
    entries = jax.random.normal(stream_key, shape, jnp.float32) * width * loudness
    return jnp.minimum(jnp.maximum(entries, -reach), reach).astype(kind)


def setup_inputs(seed: int = 0) -> dict:
    arg_keys = jax.random.split(jax.random.key(seed), 6)
    blocks = scatter_about(arg_keys[0], (N_ROW, N_COL, SLOTS, BLOCK, BLOCK), (BLOCK * SLOTS * N_COL // TILE_ROWS) ** -0.5, 0.25, ((0, 8), (1, 4)))
    block_rows = set_ends(jax.random.randint(arg_keys[1], (N_ROW, N_COL, SLOTS), 0, TILE_ROWS), jax.random.fold_in(arg_keys[1], 1), 0, TILE_ROWS - 1).astype(jnp.int32)
    block_cols = set_ends(jax.random.randint(arg_keys[2], (N_ROW, N_COL, SLOTS), 0, TILE_COLS), jax.random.fold_in(arg_keys[2], 1), 0, TILE_COLS - 1).astype(jnp.int32)
    counts = draw_counts(jax.random.fold_in(arg_keys[5], 71), 0)
    data = draw_data(jax.random.fold_in(arg_keys[5], 71), 0)
    return {"blocks": blocks, "block_rows": block_rows, "block_cols": block_cols, "counts": counts, "data": data}


EPS = 1e-06

def forward(blocks, block_rows, block_cols, counts, vector):
    vec_b = vector.astype(jnp.bfloat16).reshape(N_COL, TILE_COLS, BLOCK)
    slot_ids = jnp.arange(SLOTS, dtype=jnp.int32)

    def one_row(args):
        tile_blocks, rows_r, cols_r, count_r = args
        picked = jax.vmap(lambda piece, index: piece[index])(vec_b, cols_r)
        prod = jnp.einsum('nkij,nkj->nki', tile_blocks.astype(jnp.float32), picked.astype(jnp.float32), precision=lax.Precision.HIGHEST)
        live = (slot_ids[None, :] < count_r[:, None]).astype(jnp.float32)
        prod = prod * live[:, :, None]
        return jax.ops.segment_sum(prod.reshape(-1, BLOCK), rows_r.reshape(-1), num_segments=TILE_ROWS)
    result = lax.map(one_row, (blocks, block_rows, block_cols, counts))
    return result.reshape(-1)

def adjoint(blocks, block_rows, block_cols, counts, vector):
    vec_b = vector.astype(jnp.bfloat16).reshape(N_ROW, TILE_ROWS, BLOCK)
    slot_ids = jnp.arange(SLOTS, dtype=jnp.int32)

    def one_row(total, args):
        tile_blocks, rows_r, cols_r, count_r, piece_r = args
        picked = piece_r[rows_r]
        prod = jnp.einsum('nkij,nki->nkj', tile_blocks.astype(jnp.float32), picked.astype(jnp.float32), precision=lax.Precision.HIGHEST)
        live = (slot_ids[None, :] < count_r[:, None]).astype(jnp.float32)
        prod = prod * live[:, :, None]
        summed = jax.vmap(lambda p, c: jax.ops.segment_sum(p, c, num_segments=TILE_COLS))(prod, cols_r)
        return (total + summed, None)
    start = jnp.zeros((N_COL, TILE_COLS, BLOCK), jnp.float32)
    total, unused = lax.scan(one_row, start, (blocks, block_rows, block_cols, counts, vec_b))
    return total.reshape(-1)

def norm(vector):
    return jnp.sqrt(jnp.sum(vector * vector) + EPS)

def reference(blocks, block_rows, block_cols, counts, data):
    beta = norm(data)
    data_basis = data / beta
    temp = adjoint(blocks, block_rows, block_cols, counts, data_basis)
    alpha = norm(temp)
    model_basis = temp / alpha
    search = model_basis
    solution = jnp.zeros_like(model_basis)
    phibar = beta
    rhobar = alpha
    for step in range(ITERS):
        temp = forward(blocks, block_rows, block_cols, counts, model_basis) - alpha * data_basis
        beta = norm(temp)
        data_basis = temp / beta
        temp = adjoint(blocks, block_rows, block_cols, counts, data_basis) - beta * model_basis
        alpha = norm(temp)
        model_basis = temp / alpha
        rho = jnp.sqrt(rhobar * rhobar + beta * beta)
        cosine = rhobar / rho
        sine = beta / rho
        theta = sine * alpha
        rhobar = -cosine * alpha
        phi = cosine * phibar
        phibar = sine * phibar
        solution = solution + phi / rho * search
        search = model_basis - theta / rho * search
    return (solution, search, data_basis)
```

```python
import functools

import jax
import jax.numpy as jnp
from jax import lax
from jax.experimental import pallas as pl
from jax.experimental.pallas import tpu as pltpu
from jax.sharding import PartitionSpec as P

TILE_COLS = 256
ITERS = 3
EPS = 1e-06
GROUP = 16
RIDE = 8


def halves(values):
    high = values.astype(jnp.bfloat16)
    low = (values - high.astype(jnp.float32)).astype(jnp.bfloat16)
    return jnp.concatenate([high, low], 0)


def squares(vector):
    rows, width = vector.shape
    return jnp.sum((vector * vector).reshape(rows // RIDE, RIDE, width), 0)


def norm_row(tile):
    total = jnp.sum(jnp.sum(tile, 0, keepdims=True), 1, keepdims=True)
    return jnp.broadcast_to(jnp.sqrt(total + EPS), (1, tile.shape[1]))


def slot_products(pick_ref, vector, blocks_ref, picked_ref, prod_ref, transpose):
    picked_ref[...] = jnp.dot(
        pick_ref[...], vector.astype(jnp.bfloat16), preferred_element_type=jnp.float32
    ).astype(jnp.bfloat16)
    slots, width, _ = blocks_ref.shape
    if transpose:
        shape = (GROUP, GROUP * width)
        mine = lax.broadcasted_iota(jnp.int32, shape, 1) // width == lax.broadcasted_iota(jnp.int32, shape, 0)
    else:
        row = lax.broadcasted_iota(jnp.int32, (GROUP, width), 0)
    for at in range(0, slots, GROUP):
        piece = picked_ref[at : at + GROUP]
        stack = blocks_ref[at : at + GROUP].reshape(GROUP * width, width)
        if transpose:
            spread = jnp.where(mine, jnp.concatenate([piece] * GROUP, 1), jnp.bfloat16(0))
            prod_ref[at : at + GROUP] = jnp.dot(spread, stack, preferred_element_type=jnp.float32)
        else:
            every = lax.dot_general(
                piece, stack, (((1,), (1,)), ((), ())), preferred_element_type=jnp.float32
            )
            total = jnp.zeros((GROUP, width), jnp.float32)
            for slot in range(GROUP):
                total = total + jnp.where(row == slot, every[:, slot * width : (slot + 1) * width], 0.0)
            prod_ref[at : at + GROUP] = total


def send(put_ref, vector, prod_ref, out_ref):
    put = put_ref[...]
    rows = put.shape[0]
    out_ref[:rows] = jnp.dot(
        jnp.concatenate([put, put], 1), halves(prod_ref[...]), preferred_element_type=jnp.float32
    )
    out_ref[rows:] = squares(vector)


def first_kernel(pick_ref, put_ref, data_ref, blocks_ref, out_ref, picked_ref, prod_ref):
    vector = data_ref[...]
    slot_products(pick_ref, vector, blocks_ref, picked_ref, prod_ref, True)
    send(put_ref, vector, prod_ref, out_ref)


def recur(summed_ref, previous):
    rows = summed_ref.shape[0] - RIDE
    norm = norm_row(summed_ref[rows:])
    vector = summed_ref[:rows] * (1.0 / norm)
    if previous:
        before_ref, before_norm_ref = previous
        vector = vector - (norm / before_norm_ref[:1]) * before_ref[...]
    return vector, norm


def step_kernel(transpose, pick_ref, put_ref, summed_ref, *refs):
    *previous, blocks_ref, out_ref, vector_ref, norm_ref, picked_ref, prod_ref = refs
    vector, norm = recur(summed_ref, previous)
    vector_ref[...] = vector
    norm_ref[...] = jnp.broadcast_to(norm, norm_ref.shape)
    slot_products(pick_ref, vector, blocks_ref, picked_ref, prod_ref, transpose)
    send(put_ref, vector, prod_ref, out_ref)


def last_kernel(steps, summed_ref, data_vector_ref, *refs):
    norms, refs = refs[: 2 * steps], refs[2 * steps :]
    alphas, betas = [r[:1] for r in norms[:steps]], [r[:1] for r in norms[steps:]]
    models, (solution_ref, search_ref, vector_ref, basis_ref, square_ref, coef_ref) = refs[:steps], refs[steps:]
    vector, beta = recur(summed_ref, (models[-1], norms[steps - 1]))
    betas.append(beta)
    vector_ref[...] = vector
    square_ref[...] = squares(vector)
    basis_ref[...] = data_vector_ref[...] * (1.0 / beta)
    search = models[0][...] * (1.0 / alphas[0])
    solution = jnp.zeros_like(search)
    phibar, rhobar = betas[0], alphas[0]
    for step in range(steps):
        rho = jnp.sqrt(rhobar * rhobar + betas[step + 1] * betas[step + 1])
        cosine, sine = rhobar / rho, betas[step + 1] / rho
        solution = solution + (cosine * phibar / rho) * search
        phibar = sine * phibar
        if step + 1 < steps:
            rhobar = -cosine * alphas[step + 1]
            search = models[step + 1][...] * (1.0 / alphas[step + 1]) - (sine * alphas[step + 1] / rho) * search
    solution_ref[...] = solution
    search_ref[...] = search
    coef_ref[...] = jnp.broadcast_to(sine / rho, coef_ref.shape)


def search_kernel(square_ref, vector_ref, search_ref, coef_ref, out_ref):
    alpha = norm_row(square_ref[...])
    out_ref[...] = vector_ref[...] * (1.0 / alpha) - (coef_ref[:1] * alpha) * search_ref[...]


def call(kernel, outs, args, slots=None, width=None):
    spec = pl.BlockSpec(memory_space=pltpu.VMEM)
    scratch = [] if slots is None else [pltpu.VMEM((slots, width), jnp.bfloat16), pltpu.VMEM((slots, width), jnp.float32)]
    return pl.pallas_call(
        kernel,
        out_shape=[jax.ShapeDtypeStruct(shape, jnp.float32) for shape in outs],
        in_specs=[spec] * len(args),
        out_specs=[spec] * len(outs),
        scratch_shapes=scratch,
        compiler_params=pltpu.CompilerParams(vmem_limit_bytes=32 * 1024 * 1024),
    )(*args)


def all_sum(values, axis, size):
    bit = 1
    while bit < size:
        values = values + lax.ppermute(values, axis, [(i, i ^ bit) for i in range(size)])
        bit *= 2
    return values


def per_device(n_row, n_col, blocks, block_rows, block_cols, counts, data):
    tile_blocks = blocks[0, 0]
    slots, _, width = tile_blocks.shape
    data = data.reshape(-1, width)
    tile_rows, tile_cols = data.shape[0], TILE_COLS
    live = jnp.arange(slots, dtype=jnp.int32) < counts[0, 0]

    def picks(index, size):
        index = jnp.where(live, index, -1)
        places = jnp.arange(size, dtype=jnp.int32)
        pick = (index[:, None] == places[None, :]).astype(jnp.bfloat16)
        put = (places[:, None] == index[None, :]).astype(jnp.bfloat16)
        return pick, put

    pick_row, put_row = picks(block_rows[0, 0], tile_rows)
    pick_col, put_col = picks(block_cols[0, 0], tile_cols)
    tile, model, basis = (RIDE, width), (tile_cols, width), (tile_rows, width)
    to_model, to_basis = (tile_cols + RIDE, width), (tile_rows + RIDE, width)
    (part,) = call(first_kernel, [to_model], [pick_row, put_col, data, tile_blocks], slots, width)
    summed = all_sum(part, "row", n_row)
    alphas, betas, models = [], [], []
    bases = [data]
    for step in range(ITERS):
        previous = [models[-1], alphas[-1]] if models else []
        part, vector, beta = call(
            functools.partial(step_kernel, False),
            [to_basis, model, tile],
            [pick_col, put_row, summed, *previous, tile_blocks],
            slots,
            width,
        )
        models.append(vector)
        betas.append(beta)
        summed = all_sum(part, "col", n_col)
        part, vector, alpha = call(
            functools.partial(step_kernel, True),
            [to_model, basis, tile],
            [pick_row, put_col, summed, bases[-1], beta, tile_blocks],
            slots,
            width,
        )
        bases.append(vector)
        alphas.append(alpha)
        summed = all_sum(part, "row", n_row)
    solution, search, vector, data_basis, square, coef = call(
        functools.partial(last_kernel, ITERS),
        [model, model, model, basis, tile, tile],
        [summed, bases[-1], *alphas, *betas, *models],
    )
    square = all_sum(square, "col", n_col)
    (search,) = call(search_kernel, [model], [square, vector, search, coef])
    return solution.reshape(-1), search.reshape(-1), data_basis.reshape(-1)


def solution(mesh):
    in_specs = (
        P("row", "col", None, None, None),
        P("row", "col", None),
        P("row", "col", None),
        P("row", "col"),
        P("row"),
    )
    out_specs = (P("col"), P("col"), P("row"))
    return jax.shard_map(
        functools.partial(per_device, mesh.shape["row"], mesh.shape["col"]),
        mesh=mesh,
        in_specs=in_specs,
        out_specs=out_specs,
        check_vma=False,
    )
```

```python
import functools

import jax
import jax.numpy as jnp
from jax import lax
from jax.experimental import pallas as pl
from jax.experimental.pallas import tpu as pltpu
from jax.sharding import PartitionSpec as P

TILE_COLS = 256
ITERS = 3
EPS = 1e-06
VMEM_LIMIT = 4 * 1024 * 1024
GROUP = 16
FLIPS = 4
LOADS = (8, 6, 2)
AHEAD = 2
RIDE = 8


def halves(values):
    high = values.astype(jnp.bfloat16)
    low = (values - high.astype(jnp.float32)).astype(jnp.bfloat16)
    return jnp.concatenate([high, low], 0)


def squares(vector):
    rows, width = vector.shape
    return jnp.sum((vector * vector).reshape(rows // RIDE, RIDE, width), 0)


def norm_row(tile):
    total = jnp.sum(jnp.sum(tile, 0, keepdims=True), 1, keepdims=True)
    return jnp.broadcast_to(jnp.sqrt(total + EPS), (1, tile.shape[1]))


def slot_products(pick, vector, blocks_refs, picked_ref, prod_ref, ready=None):
    picked_ref[...] = jnp.dot(
        pick, vector.astype(jnp.bfloat16), preferred_element_type=jnp.float32
    ).astype(jnp.bfloat16)
    slots, width = picked_ref.shape
    shape = (GROUP, GROUP * width)
    mine = lax.broadcasted_iota(jnp.int32, shape, 1) // width == lax.broadcasted_iota(jnp.int32, shape, 0)
    share = blocks_refs[0].shape[0]
    for at in range(0, slots, GROUP):
        if ready:
            ready(at)
        piece = picked_ref[at : at + GROUP]
        spread = jnp.where(mine, jnp.concatenate([piece] * GROUP, 1), jnp.bfloat16(0))
        here = pl.ds(at % share, GROUP)
        stack = blocks_refs[at // share][here].reshape(GROUP * width, width)
        prod_ref[at : at + GROUP] = jnp.dot(spread, stack, preferred_element_type=jnp.float32)


def send(put_ref, vector, prod_ref, out_refs):
    top_ref, low_ref = out_refs
    put = put_ref[...]
    rows, top = put.shape[0], top_ref.shape[0]
    part = jnp.dot(
        jnp.concatenate([put, put], 1), halves(prod_ref[...]), preferred_element_type=jnp.float32
    )
    top_ref[...] = part[:top]
    low_ref[: rows - top] = part[top:]
    low_ref[rows - top :] = squares(vector)


def first_kernel(
    rows_hbm, cols_hbm, count_ref, data_hbm, blocks_hbm,
    top_ref, low_ref, data_ref, pick_row_ref, put_row_ref, pick_col_ref, put_col_ref, blocks_ref,
    picked_ref, prod_ref, rows_ref, cols_ref, small_sems, block_sems,
):
    slots = blocks_ref.shape[0]
    starts = [slots * sum(LOADS[:part]) // sum(LOADS) for part in range(len(LOADS))]
    small = []
    for at, pair in enumerate(((rows_hbm, rows_ref), (cols_hbm, cols_ref), (data_hbm, data_ref))):
        small.append(pltpu.make_async_copy(*pair, small_sems.at[at]))
        small[-1].start()
    copies = []
    for part, start in enumerate(starts):
        piece = pl.ds(start, slots * LOADS[part] // sum(LOADS))
        copies.append(pltpu.make_async_copy(blocks_hbm.at[piece], blocks_ref.at[piece], block_sems.at[part]))
    for copy in copies[:AHEAD]:
        copy.start()
    for copy, index_ref, pick_ref, put_ref in (
        (small[0], rows_ref, pick_row_ref, put_row_ref),
        (small[1], cols_ref, pick_col_ref, put_col_ref),
    ):
        copy.wait()
        shape = put_ref.shape
        live = lax.broadcasted_iota(jnp.int32, shape, 1) < count_ref[0, 0]
        chosen = (lax.broadcasted_iota(jnp.int32, shape, 0) == index_ref[...]) & live
        put = jnp.where(chosen, 1.0, 0.0)
        put_ref[...] = put.astype(jnp.bfloat16)
        pick_ref[...] = put.T.astype(jnp.bfloat16)
    small[2].wait()
    vector = data_ref[...]

    def ready(at):
        if at in starts:
            part = starts.index(at)
            copies[part].wait()
            for copy in copies[part + AHEAD : part + AHEAD + 1]:
                copy.start()

    slot_products(pick_row_ref[...], vector, [blocks_ref], picked_ref, prod_ref, ready)
    send(put_col_ref, vector, prod_ref, (top_ref, low_ref))


def flip_kernel(first, blocks_ref, flipped_ref):
    for slot in range(flipped_ref.shape[0]):
        flipped_ref[slot] = blocks_ref[first + slot].T


def recur(summed_refs, previous):
    top_ref, low_ref = summed_refs
    rows = low_ref.shape[0] - RIDE
    norm = norm_row(low_ref[rows:])
    vector = jnp.concatenate([top_ref[...], low_ref[:rows]], 0) * (1.0 / norm)
    if previous:
        before_ref, before_norm_ref = previous
        vector = vector - (norm / before_norm_ref[:1]) * before_ref[...]
    return vector, norm


def step_kernel(pieces, pick_ref, put_ref, top_in_ref, low_in_ref, *refs):
    blocks_refs, refs = refs[:pieces], refs[pieces:]
    *previous, top_ref, low_ref, vector_ref, norm_ref, picked_ref, prod_ref = refs
    vector, norm = recur((top_in_ref, low_in_ref), previous)
    vector_ref[...] = vector
    norm_ref[...] = jnp.broadcast_to(norm, norm_ref.shape)
    slot_products(pick_ref[...], vector, blocks_refs, picked_ref, prod_ref)
    send(put_ref, vector, prod_ref, (top_ref, low_ref))


def end_kernel(top_in_ref, low_in_ref, before_ref, before_norm_ref, square_ref, vector_ref, norm_ref):
    vector, norm = recur((top_in_ref, low_in_ref), (before_ref, before_norm_ref))
    square_ref[...] = squares(vector)
    vector_ref[...] = vector
    norm_ref[...] = jnp.broadcast_to(norm, norm_ref.shape)


def update_kernel(steps, data_vector_ref, *refs):
    alphas, refs = [r[:1] for r in refs[:steps]], refs[steps:]
    betas, refs = [r[:1] for r in refs[: steps + 1]], refs[steps + 1 :]
    models, (solution_ref, search_ref, basis_ref, coef_ref) = refs[:steps], refs[steps:]
    basis_ref[...] = data_vector_ref[...] * (1.0 / betas[-1])
    search = models[0][...] * (1.0 / alphas[0])
    solution = jnp.zeros_like(search)
    phibar, rhobar = betas[0], alphas[0]
    for step in range(steps):
        rho = jnp.sqrt(rhobar * rhobar + betas[step + 1] * betas[step + 1])
        cosine, sine = rhobar / rho, betas[step + 1] / rho
        solution = solution + (cosine * phibar / rho) * search
        phibar = sine * phibar
        if step + 1 < steps:
            rhobar = -cosine * alphas[step + 1]
            search = models[step + 1][...] * (1.0 / alphas[step + 1]) - (sine * alphas[step + 1] / rho) * search
    solution_ref[...] = solution
    search_ref[...] = search
    coef_ref[...] = jnp.broadcast_to(sine / rho, coef_ref.shape)


def search_kernel(square_ref, vector_ref, search_ref, coef_ref, out_ref):
    alpha = norm_row(square_ref[...])
    out_ref[...] = vector_ref[...] * (1.0 / alpha) - (coef_ref[:1] * alpha) * search_ref[...]


VMEM = pl.BlockSpec(memory_space=pltpu.VMEM)


def call(kernel, outs, args, scratch=(), specs=None):
    return pl.pallas_call(
        kernel,
        out_shape=[jax.ShapeDtypeStruct(o, jnp.float32) if isinstance(o, tuple) else o for o in outs],
        in_specs=specs or [VMEM] * len(args),
        out_specs=[VMEM] * len(outs),
        scratch_shapes=list(scratch),
        cost_estimate=pl.CostEstimate(flops=2 * 10**9, bytes_accessed=2**20, transcendentals=0),
        compiler_params=pltpu.CompilerParams(vmem_limit_bytes=VMEM_LIMIT),
    )(*args)


def all_sum(chunks, orders, axis, size):
    chunks = list(chunks)
    for stage in range(len(orders[0])):
        for at, order in enumerate(orders):
            pairs = [(i, i ^ order[stage]) for i in range(size)]
            chunks[at] = chunks[at] + lax.ppermute(chunks[at], axis, pairs)
    return chunks


def per_device(n_row, n_col, blocks, block_rows, block_cols, counts, data):
    tile_blocks = blocks[0, 0]
    slots, _, width = tile_blocks.shape
    data = data.reshape(-1, width)
    tile_rows, tile_cols = data.shape[0], TILE_COLS
    row_bits = [1 << k for k in range(n_row.bit_length() - 1)]
    col_bits = [1 << k for k in range(n_col.bit_length() - 1)]
    row_orders, col_orders = [row_bits, row_bits], [col_bits[::-1], col_bits]
    tile, model, basis = (RIDE, width), (tile_cols, width), (tile_rows, width)

    def chunks(rows):
        return [(rows // 2, width), (rows - rows // 2 + RIDE, width)]

    def coded(*shape):
        return jax.ShapeDtypeStruct(shape, jnp.bfloat16)

    scratch = [pltpu.VMEM((slots, width), jnp.bfloat16), pltpu.VMEM((slots, width), jnp.float32)]
    hbm = pl.BlockSpec(memory_space=pltpu.HBM)
    inputs = [
        pltpu.with_memory_space_constraint(a, pltpu.HBM) for a in (block_rows[0], block_cols[0], data, tile_blocks)
    ]
    *parts, data, pick_row, put_row, pick_col, put_col, tile_blocks = call(
        first_kernel,
        [
            *chunks(tile_cols), basis, coded(slots, tile_rows), coded(tile_rows, slots),
            coded(slots, tile_cols), coded(tile_cols, slots),
            coded(*tile_blocks.shape),
        ],
        [inputs[0], inputs[1], counts, inputs[2], inputs[3]],
        [
            *scratch, pltpu.VMEM((1, slots), jnp.int32), pltpu.VMEM((1, slots), jnp.int32),
            pltpu.SemaphoreType.DMA((3,)), pltpu.SemaphoreType.DMA((len(LOADS),)),
        ],
        [hbm, hbm, pl.BlockSpec(memory_space=pltpu.SMEM), hbm, hbm],
    )
    share = slots // FLIPS
    flipped = [
        call(functools.partial(flip_kernel, at * share), [coded(share, width, width)], [tile_blocks])[0]
        for at in range(FLIPS)
    ]
    summed = all_sum(parts, row_orders, "row", n_row)
    alphas, betas, models = [], [], []
    bases = [data]
    for step in range(ITERS):
        previous = [models[-1], alphas[-1]] if models else []
        *parts, vector, beta = call(
            functools.partial(step_kernel, FLIPS),
            [*chunks(tile_rows), model, tile],
            [pick_col, put_row, *summed, *flipped, *previous],
            scratch,
        )
        models.append(vector)
        betas.append(beta)
        summed = all_sum(parts, col_orders, "col", n_col)
        *parts, vector, alpha = call(
            functools.partial(step_kernel, 1),
            [*chunks(tile_cols), basis, tile],
            [pick_row, put_col, *summed, tile_blocks, bases[-1], beta],
            scratch,
        )
        bases.append(vector)
        alphas.append(alpha)
        summed = all_sum(parts, row_orders, "row", n_row)
    square, vector, beta = call(end_kernel, [tile, model, tile], [*summed, models[-1], alphas[-1]])
    solution, search, data_basis, coef = call(
        functools.partial(update_kernel, ITERS),
        [model, model, basis, tile],
        [bases[-1], *alphas, *betas, beta, *models],
    )
    (square,) = all_sum([square], [col_bits], "col", n_col)
    (search,) = call(search_kernel, [model], [square, vector, search, coef])
    return solution.reshape(-1), search.reshape(-1), data_basis.reshape(-1)


def solution(mesh):
    in_specs = (
        P("row", "col", None, None, None),
        P("row", "col", None),
        P("row", "col", None),
        P("row", "col"),
        P("row"),
    )
    out_specs = (P("col"), P("col"), P("row"))
    return jax.shard_map(
        functools.partial(per_device, mesh.shape["row"], mesh.shape["col"]),
        mesh=mesh,
        in_specs=in_specs,
        out_specs=out_specs,
        check_vma=False,
    )
```

```python
import functools

import jax
import jax.numpy as jnp
from jax import lax
from jax.experimental import pallas as pl
from jax.experimental.pallas import tpu as pltpu
from jax.sharding import PartitionSpec as P


TILE_COLS = 256
ITERS = 3
EPS = 1e-06
VMEM_LIMIT = 4 * 1024 * 1024
GROUP = 16
PIECES = 2
LOADS = (8, 6, 2)
AHEAD = 2
TURNS = {"row": (1, 0), "col": (1, 0)}
RIDE = 8


def halves(values):
    high = values.astype(jnp.bfloat16)
    low = (values - high.astype(jnp.float32)).astype(jnp.bfloat16)
    return jnp.concatenate([high, low], 0)


def squares(vector):
    rows, width = vector.shape
    return jnp.sum((vector * vector).reshape(rows // RIDE, RIDE, width), 0)


def norm_row(tile):
    total = jnp.sum(jnp.sum(tile, 0, keepdims=True), 1, keepdims=True)
    return jnp.broadcast_to(jnp.sqrt(total + EPS), (1, tile.shape[1]))


def pick_pieces(pick, vector):
    return jnp.dot(
        pick, vector.astype(jnp.bfloat16), preferred_element_type=jnp.float32
    ).astype(jnp.bfloat16)


def group_products(picked, stack):
    group, width = picked.shape
    shape = (group, group * width)
    mine = lax.broadcasted_iota(jnp.int32, shape, 1) // width == lax.broadcasted_iota(jnp.int32, shape, 0)
    spread = jnp.where(mine, jnp.concatenate([picked] * group, 1), jnp.bfloat16(0))
    return jnp.dot(spread, stack.reshape(group * width, width), preferred_element_type=jnp.float32)


def put_products(put, products):
    return jnp.dot(
        jnp.concatenate([put, put], 1), halves(products), preferred_element_type=jnp.float32
    )


def first_kernel(
    rows_hbm, cols_hbm, count_ref, data_hbm, blocks_hbm,
    top_ref, low_ref, data_ref, pick_row_ref, put_row_ref, pick_col_ref, put_col_ref, order_ref, number_f_ref, number_a_ref, blocks_ref,
    prod_ref, rows_ref, cols_ref, small_sems, block_sems,
):
    slots = blocks_ref.shape[0]
    starts = [slots * sum(LOADS[:part]) // sum(LOADS) for part in range(len(LOADS))]
    small = []
    for at, pair in enumerate(((rows_hbm, rows_ref), (cols_hbm, cols_ref), (data_hbm, data_ref))):
        small.append(pltpu.make_async_copy(*pair, small_sems.at[at]))
        small[-1].start()
    copies = []
    for part, start in enumerate(starts):
        piece = pl.ds(start, slots * LOADS[part] // sum(LOADS))
        copies.append(pltpu.make_async_copy(blocks_hbm.at[piece], blocks_ref.at[piece], block_sems.at[part]))
    for copy in copies[:AHEAD]:
        copy.start()
    square = (slots, slots)
    slot = lax.broadcasted_iota(jnp.int32, (1, slots), 1)
    down = lax.broadcasted_iota(jnp.int32, square, 0)
    live = slot < count_ref[0, 0]

    def one_hot(index_ref, size):
        places = lax.broadcasted_iota(jnp.int32, (size, slots), 0)
        put = jnp.where((places == index_ref[...]) & live, 1.0, 0.0)
        return put.T.astype(jnp.bfloat16), put.astype(jnp.bfloat16)

    def ordered(index_ref, size):
        late = index_ref[...] < size // 2
        key = (jnp.where(live, jnp.where(late, 2, 0), 1) * slots + slot).astype(jnp.float32)
        keys = jnp.broadcast_to(key, square)
        place = jnp.sum(jnp.where(keys.T < keys, 1.0, 0.0), 0, keepdims=True).astype(jnp.int32)
        moved = jnp.where(down == place, 1.0, 0.0).astype(jnp.bfloat16)
        ids = jnp.broadcast_to(slot, (RIDE, slots)).astype(jnp.float32).astype(jnp.bfloat16)
        order = lax.dot_general(ids, moved, (((1,), (1,)), ((), ())), preferred_element_type=jnp.float32)
        number = jnp.sum(jnp.where(live & late, 1.0, 0.0), 1, keepdims=True)
        return moved, order[:1].astype(jnp.int32), jnp.broadcast_to(number, number_f_ref.shape).astype(jnp.int32)

    for copy in small[:2]:
        copy.wait()
    sizes = data_ref.shape[0], put_col_ref.shape[0]
    pick_row, put_row = one_hot(rows_ref, sizes[0])
    pick_col, put_col = one_hot(cols_ref, sizes[1])
    moved_f, order_ref[:1], number_f_ref[...] = ordered(cols_ref, sizes[1])
    moved_a, order_ref[1:], number_a_ref[...] = ordered(rows_ref, sizes[0])
    for moved, pick, put, to_pick_ref, to_put_ref in (
        (moved_f, pick_col, put_row, pick_col_ref, put_row_ref),
        (moved_a, pick_row, put_col, pick_row_ref, put_col_ref),
    ):
        to_pick_ref[...] = jnp.dot(moved, pick, preferred_element_type=jnp.float32).astype(jnp.bfloat16)
        to_put_ref[...] = lax.dot_general(
            put, moved, (((1,), (1,)), ((), ())), preferred_element_type=jnp.float32
        ).astype(jnp.bfloat16)
    small[2].wait()
    vector = data_ref[...]
    picked = pick_pieces(pick_row, vector)
    for at in range(0, slots, GROUP):
        if at in starts:
            part = starts.index(at)
            copies[part].wait()
            for copy in copies[part + AHEAD : part + AHEAD + 1]:
                copy.start()
        here = slice(at, at + GROUP)
        prod_ref[here] = group_products(picked[here], blocks_ref[here])
    part = put_products(put_col, prod_ref[...])
    rows, top = part.shape[0], top_ref.shape[0]
    top_ref[...] = part[:top]
    low_ref[: rows - top] = part[top:]
    low_ref[rows - top :] = squares(vector)


def arrange_kernel(first, order_ref, blocks_ref, plain_ref, flipped_ref):
    for slot in range(flipped_ref.shape[0]):
        flipped_ref[slot] = blocks_ref[order_ref[0, first + slot]].T
        plain_ref[slot] = blocks_ref[order_ref[1, first + slot]]


def recur(summed, norm, previous, here):
    vector = summed * (1.0 / norm)
    if previous:
        before_ref, before_norm_ref = previous
        vector = vector - (norm / before_norm_ref[:1]) * before_ref[here]
    return vector


def stack_of(blocks_refs, at):
    share = blocks_refs[0].shape[0]
    return blocks_refs[at // share][at % share : at % share + GROUP]


def early_kernel(pieces, pick_ref, low_in_ref, *refs):
    blocks_refs, refs = refs[:pieces], refs[pieces:]
    *previous, vector_ref, norm_ref, early_ref = refs
    rows, early = vector_ref.shape[0], early_ref.shape[0]
    norm = norm_row(low_in_ref[rows:])
    norm_ref[...] = jnp.broadcast_to(norm, norm_ref.shape)
    size = pick_ref.shape[1]
    vector = recur(low_in_ref[:rows], norm, previous, slice(size - rows, size))
    vector_ref[...] = vector
    picked = pick_pieces(pick_ref[:early, size - rows :], vector)
    for at in range(0, early, GROUP):
        early_ref[at : at + GROUP] = group_products(picked[at : at + GROUP], stack_of(blocks_refs, at))


def rest_kernel(pieces, number_ref, pick_ref, put_ref, top_in_ref, low_vector_ref, norm_ref, early_ref, *refs):
    blocks_refs, refs = refs[:pieces], refs[pieces:]
    *previous, top_ref, low_ref, vector_ref, picked_ref, prod_ref = refs
    top = top_in_ref.shape[0]
    vector_ref[:top] = recur(top_in_ref[...], norm_ref[:1], previous, slice(0, top))
    vector_ref[top:] = low_vector_ref[...]
    vector = vector_ref[...]
    slots, early, share = pick_ref.shape[0], early_ref.shape[0], blocks_refs[0].shape[0]
    picked_ref[...] = pick_pieces(pick_ref[...], vector)
    prod_ref[:early] = early_ref[...]
    for at in range(early, slots, GROUP):
        prod_ref[at : at + GROUP] = group_products(picked_ref[at : at + GROUP], stack_of(blocks_refs, at))

    @pl.when(jnp.max(number_ref[...]) > slots - early)
    def _():
        for piece, blocks_ref in enumerate(blocks_refs[: pl.cdiv(early, share)]):

            @pl.loop(0, min(share, early - piece * share) // GROUP)
            def _(group):
                at = pl.multiple_of(group * GROUP, GROUP)
                here = pl.ds(pl.multiple_of(piece * share + at, GROUP), GROUP)
                prod_ref[here] = group_products(picked_ref[here], blocks_ref[pl.ds(at, GROUP)])

    part = put_products(put_ref[...], prod_ref[...])
    rows, top = part.shape[0], top_ref.shape[0]
    top_ref[...] = part[:top]
    low_ref[: rows - top] = part[top:]
    low_ref[rows - top :] = squares(vector)


def end_kernel(top_in_ref, low_in_ref, before_ref, before_norm_ref, square_ref, vector_ref, norm_ref):
    rows = low_in_ref.shape[0] - RIDE
    norm = norm_row(low_in_ref[rows:])
    summed = jnp.concatenate([top_in_ref[...], low_in_ref[:rows]], 0)
    vector = recur(summed, norm, (before_ref, before_norm_ref), slice(None))
    square_ref[...] = squares(vector)
    vector_ref[...] = vector
    norm_ref[...] = jnp.broadcast_to(norm, norm_ref.shape)


def update_kernel(steps, data_vector_ref, *refs):
    alphas, refs = [r[:1] for r in refs[:steps]], refs[steps:]
    betas, refs = [r[:1] for r in refs[: steps + 1]], refs[steps + 1 :]
    models, (solution_ref, search_ref, basis_ref, coef_ref) = refs[:steps], refs[steps:]
    basis_ref[...] = data_vector_ref[...] * (1.0 / betas[-1])
    search = models[0][...] * (1.0 / alphas[0])
    solution = jnp.zeros_like(search)
    phibar, rhobar = betas[0], alphas[0]
    for step in range(steps):
        rho = jnp.sqrt(rhobar * rhobar + betas[step + 1] * betas[step + 1])
        cosine, sine = rhobar / rho, betas[step + 1] / rho
        solution = solution + (cosine * phibar / rho) * search
        phibar = sine * phibar
        if step + 1 < steps:
            rhobar = -cosine * alphas[step + 1]
            search = models[step + 1][...] * (1.0 / alphas[step + 1]) - (sine * alphas[step + 1] / rho) * search
    solution_ref[...] = solution
    search_ref[...] = search
    coef_ref[...] = jnp.broadcast_to(sine / rho, coef_ref.shape)


def search_kernel(square_ref, vector_ref, search_ref, coef_ref, out_ref):
    alpha = norm_row(square_ref[...])
    out_ref[...] = vector_ref[...] * (1.0 / alpha) - (coef_ref[:1] * alpha) * search_ref[...]


VMEM = pl.BlockSpec(memory_space=pltpu.VMEM)


def call(kernel, outs, args, scratch=(), specs=None):
    return pl.pallas_call(
        kernel,
        out_shape=[jax.ShapeDtypeStruct(o, jnp.float32) if isinstance(o, tuple) else o for o in outs],
        in_specs=specs or [VMEM] * len(args),
        out_specs=[VMEM] * len(outs),
        scratch_shapes=list(scratch),
        cost_estimate=pl.CostEstimate(flops=2 * 10**9, bytes_accessed=2**20, transcendentals=0),
        compiler_params=pltpu.CompilerParams(vmem_limit_bytes=VMEM_LIMIT),
    )(*args)


def all_sum(chunks, orders, turns, axis, size):
    chunks = list(chunks)
    stages = len(orders[0])
    for stage in range(stages):
        for at in turns:
            pairs = [(i, i ^ orders[at][stage]) for i in range(size)]
            other = lax.ppermute(chunks[at], axis, pairs)
            chunks[at] = chunks[at] + other
    return chunks


def per_device(n_row, n_col, blocks, block_rows, block_cols, counts, data):
    tile_blocks = blocks[0, 0]
    slots, _, width = tile_blocks.shape
    data = data.reshape(-1, width)
    tile_rows, tile_cols = data.shape[0], TILE_COLS
    row_bits = [1 << k for k in range(n_row.bit_length() - 1)]
    col_bits = [1 << k for k in range(n_col.bit_length() - 1)]
    row_orders, col_orders = [row_bits, row_bits], [col_bits[::-1], col_bits]
    tile, model, basis = (RIDE, width), (tile_cols, width), (tile_rows, width)

    def chunks(rows):
        return [(rows // 2, width), (rows - rows // 2 + RIDE, width)]

    def coded(*shape):
        return jax.ShapeDtypeStruct(shape, jnp.bfloat16)

    products = pltpu.VMEM((slots, width), jnp.float32)
    hbm, smem = pl.BlockSpec(memory_space=pltpu.HBM), pl.BlockSpec(memory_space=pltpu.SMEM)
    inputs = [
        pltpu.with_memory_space_constraint(a, pltpu.HBM) for a in (block_rows[0], block_cols[0], data, tile_blocks)
    ]
    *parts, data, pick_row, put_row, pick_col, put_col, order, number_f, number_a, tile_blocks = call(
        first_kernel,
        [
            *chunks(tile_cols), basis, coded(slots, tile_rows), coded(tile_rows, slots),
            coded(slots, tile_cols), coded(tile_cols, slots),
            *[jax.ShapeDtypeStruct(shape, jnp.int32) for shape in ((2, slots), tile, tile)], coded(*tile_blocks.shape),
        ],
        [inputs[0], inputs[1], counts, inputs[2], inputs[3]],
        [
            products, pltpu.VMEM((1, slots), jnp.int32), pltpu.VMEM((1, slots), jnp.int32),
            pltpu.SemaphoreType.DMA((3,)), pltpu.SemaphoreType.DMA((len(LOADS),)),
        ],
        [hbm, hbm, smem, hbm, hbm],
    )
    share = slots // PIECES
    plain, flipped = [], []
    for at in range(PIECES):
        pieces = call(
            functools.partial(arrange_kernel, at * share),
            [coded(share, width, width)] * 2,
            [order, tile_blocks],
            specs=[smem, VMEM],
        )
        plain.append(pieces[0])
        flipped.append(pieces[1])
    early = (slots // GROUP // 2 - 1) * GROUP

    def product(number, pick, put, parts, orders, axis, size, stacks, previous, out_rows, vector_rows):
        top, low = all_sum(parts, orders, TURNS[axis], axis, size)
        low_rows = low.shape[0] - RIDE
        low_vector, norm, done = call(
            functools.partial(early_kernel, PIECES),
            [(low_rows, width), tile, (early, width)],
            [pick, low, *stacks, *previous],
        )
        *parts, vector = call(
            functools.partial(rest_kernel, PIECES),
            [*chunks(out_rows), (vector_rows, width)],
            [number, pick, put, top, low_vector, norm, done, *stacks, *previous],
            [pltpu.VMEM((slots, width), jnp.bfloat16), products],
        )
        return parts, vector, norm

    alphas, betas, models = [], [], []
    bases = [data]
    for _ in range(ITERS):
        previous = [models[-1], alphas[-1]] if models else []
        parts, vector, beta = product(
            number_f, pick_col, put_row, parts, row_orders, "row", n_row, flipped, previous, tile_rows, tile_cols
        )
        models.append(vector)
        betas.append(beta)
        parts, vector, alpha = product(
            number_a, pick_row, put_col, parts, col_orders, "col", n_col, plain,
            [bases[-1], beta], tile_cols, tile_rows,
        )
        bases.append(vector)
        alphas.append(alpha)
    summed = all_sum(parts, row_orders, TURNS["row"], "row", n_row)
    square, vector, beta = call(end_kernel, [tile, model, tile], [*summed, models[-1], alphas[-1]])
    solution, search, data_basis, coef = call(
        functools.partial(update_kernel, ITERS),
        [model, model, basis, tile],
        [bases[-1], *alphas, *betas, beta, *models],
    )
    (square,) = all_sum([square], [col_bits], [0], "col", n_col)
    (search,) = call(search_kernel, [model], [square, vector, search, coef])
    return solution.reshape(-1), search.reshape(-1), data_basis.reshape(-1)


def solution(mesh):
    in_specs = (
        P("row", "col", None, None, None),
        P("row", "col", None),
        P("row", "col", None),
        P("row", "col"),
        P("row"),
    )
    out_specs = (P("col"), P("col"), P("row"))
    return jax.shard_map(
        functools.partial(per_device, mesh.shape["row"], mesh.shape["col"]),
        mesh=mesh,
        in_specs=in_specs,
        out_specs=out_specs,
        check_vma=False,
    )
```

```python
import functools

import jax
import jax.numpy as jnp
from jax import lax
from jax.experimental import pallas as pl
from jax.experimental.pallas import tpu as pltpu
from jax.sharding import PartitionSpec as P


TILE_COLS = 256
ITERS = 3
EPS = 1e-06
VMEM_LIMIT = 4 * 1024 * 1024
GROUP = 16
PIECES = 2
LOADS = (9, 6, 1)
AHEAD = 2
TURNS = {"row": (1, 0), "col": (1, 0)}
RIDE = 8


def halves(values):
    high = values.astype(jnp.bfloat16)
    low = (values - high.astype(jnp.float32)).astype(jnp.bfloat16)
    return jnp.concatenate([high, low], 0)


def squares(vector):
    rows, width = vector.shape
    return jnp.sum((vector * vector).reshape(rows // RIDE, RIDE, width), 0)


def norm_row(tile):
    total = jnp.sum(jnp.sum(tile, 0, keepdims=True), 1, keepdims=True)
    return jnp.broadcast_to(jnp.sqrt(total + EPS), (1, tile.shape[1]))


def pick_pieces(pick, vector):
    return jnp.dot(
        pick, vector.astype(jnp.bfloat16), preferred_element_type=jnp.float32
    ).astype(jnp.bfloat16)


def group_products(picked, stack):
    group, width = picked.shape
    shape = (group, group * width)
    mine = lax.broadcasted_iota(jnp.int32, shape, 1) // width == lax.broadcasted_iota(jnp.int32, shape, 0)
    spread = jnp.where(mine, jnp.concatenate([picked] * group, 1), jnp.bfloat16(0))
    return jnp.dot(spread, stack.reshape(group * width, width), preferred_element_type=jnp.float32)


def put_products(put, products):
    return jnp.dot(
        jnp.concatenate([put, put], 1), halves(products), preferred_element_type=jnp.float32
    )


def first_kernel(
    rows_hbm, cols_hbm, count_ref, data_hbm, blocks_hbm,
    top_ref, low_ref, data_ref, pick_row_ref, put_row_ref, pick_col_ref, put_col_ref, order_ref, number_f_ref, number_a_ref, blocks_ref,
    prod_ref, rows_ref, cols_ref, small_sems, block_sems,
):
    slots = blocks_ref.shape[0]
    starts = [slots * sum(LOADS[:part]) // sum(LOADS) for part in range(len(LOADS))]
    small = []
    for at, pair in enumerate(((rows_hbm, rows_ref), (cols_hbm, cols_ref), (data_hbm, data_ref))):
        small.append(pltpu.make_async_copy(*pair, small_sems.at[at]))
        small[-1].start()
    copies = []
    for part, start in enumerate(starts):
        piece = pl.ds(start, slots * LOADS[part] // sum(LOADS))
        copies.append(pltpu.make_async_copy(blocks_hbm.at[piece], blocks_ref.at[piece], block_sems.at[part]))
    for copy in copies[:AHEAD]:
        copy.start()
    square = (slots, slots)
    slot = lax.broadcasted_iota(jnp.int32, (1, slots), 1)
    down = lax.broadcasted_iota(jnp.int32, square, 0)
    live = slot < count_ref[0, 0]

    def one_hot(index_ref, size):
        places = lax.broadcasted_iota(jnp.int32, (size, slots), 0)
        put = jnp.where((places == index_ref[...]) & live, 1.0, 0.0)
        return put.T.astype(jnp.bfloat16), put.astype(jnp.bfloat16)

    def ordered(index_ref, size):
        late = index_ref[...] < size // 2
        key = (jnp.where(live, jnp.where(late, 2, 0), 1) * slots + slot).astype(jnp.float32)
        keys = jnp.broadcast_to(key, square)
        place = jnp.sum(jnp.where(keys.T < keys, 1.0, 0.0), 0, keepdims=True).astype(jnp.int32)
        moved = jnp.where(down == place, 1.0, 0.0).astype(jnp.bfloat16)
        ids = jnp.broadcast_to(slot, (RIDE, slots)).astype(jnp.float32).astype(jnp.bfloat16)
        order = lax.dot_general(ids, moved, (((1,), (1,)), ((), ())), preferred_element_type=jnp.float32)
        number = jnp.sum(jnp.where(live & late, 1.0, 0.0), 1, keepdims=True)
        return moved, order[:1].astype(jnp.int32), jnp.broadcast_to(number, number_f_ref.shape).astype(jnp.int32)

    for copy in small[:2]:
        copy.wait()
    sizes = data_ref.shape[0], put_col_ref.shape[0]
    pick_row, put_row = one_hot(rows_ref, sizes[0])
    pick_col, put_col = one_hot(cols_ref, sizes[1])
    moved_f, order_ref[:1], number_f_ref[...] = ordered(cols_ref, sizes[1])
    moved_a, order_ref[1:], number_a_ref[...] = ordered(rows_ref, sizes[0])
    for moved, pick, put, to_pick_ref, to_put_ref in (
        (moved_f, pick_col, put_row, pick_col_ref, put_row_ref),
        (moved_a, pick_row, put_col, pick_row_ref, put_col_ref),
    ):
        to_pick_ref[...] = jnp.dot(moved, pick, preferred_element_type=jnp.float32).astype(jnp.bfloat16)
        to_put_ref[...] = lax.dot_general(
            put, moved, (((1,), (1,)), ((), ())), preferred_element_type=jnp.float32
        ).astype(jnp.bfloat16)
    small[2].wait()
    vector = data_ref[...]
    picked = pick_pieces(pick_row, vector)
    for at in range(0, slots, GROUP):
        if at in starts:
            part = starts.index(at)
            copies[part].wait()
            for copy in copies[part + AHEAD : part + AHEAD + 1]:
                copy.start()
        here = slice(at, at + GROUP)
        prod_ref[here] = group_products(picked[here], blocks_ref[here])
    part = put_products(put_col, prod_ref[...])
    rows, top = part.shape[0], top_ref.shape[0]
    top_ref[...] = part[:top]
    low_ref[: rows - top] = part[top:]
    low_ref[rows - top :] = squares(vector)


def arrange_kernel(first, order_ref, blocks_ref, plain_ref, flipped_ref):
    for slot in range(flipped_ref.shape[0]):
        flipped_ref[slot] = blocks_ref[order_ref[0, first + slot]].T
        plain_ref[slot] = blocks_ref[order_ref[1, first + slot]]


def recur(summed, norm, previous, here):
    vector = summed * (1.0 / norm)
    if previous:
        before_ref, before_norm_ref = previous
        vector = vector - (norm / before_norm_ref[:1]) * before_ref[here]
    return vector


def stack_of(blocks_refs, at):
    share = blocks_refs[0].shape[0]
    return blocks_refs[at // share][at % share : at % share + GROUP]


def early_kernel(pieces, pick_ref, low_in_ref, *refs):
    blocks_refs, refs = refs[:pieces], refs[pieces:]
    *previous, vector_ref, norm_ref, early_ref = refs
    rows, early = vector_ref.shape[0], early_ref.shape[0]
    norm = norm_row(low_in_ref[rows:])
    norm_ref[...] = jnp.broadcast_to(norm, norm_ref.shape)
    size = pick_ref.shape[1]
    vector = recur(low_in_ref[:rows], norm, previous, slice(size - rows, size))
    vector_ref[...] = vector
    picked = pick_pieces(pick_ref[:early, size - rows :], vector)
    for at in range(0, early, GROUP):
        early_ref[at : at + GROUP] = group_products(picked[at : at + GROUP], stack_of(blocks_refs, at))


def rest_kernel(pieces, number_ref, pick_ref, put_ref, top_in_ref, low_vector_ref, norm_ref, early_ref, *refs):
    blocks_refs, refs = refs[:pieces], refs[pieces:]
    *previous, top_ref, low_ref, vector_ref, picked_ref, prod_ref = refs
    top = top_in_ref.shape[0]
    vector_ref[:top] = recur(top_in_ref[...], norm_ref[:1], previous, slice(0, top))
    vector_ref[top:] = low_vector_ref[...]
    vector = vector_ref[...]
    slots, early, share = pick_ref.shape[0], early_ref.shape[0], blocks_refs[0].shape[0]
    picked = pick_pieces(pick_ref[early:], vector)
    prod_ref[:early] = early_ref[...]
    for at in range(early, slots, GROUP):
        here = slice(at - early, at - early + GROUP)
        prod_ref[at : at + GROUP] = group_products(picked[here], stack_of(blocks_refs, at))

    def put():
        part = put_products(put_ref[...], prod_ref[...])
        rows = part.shape[0]
        top_ref[...] = part[: top_ref.shape[0]]
        low_ref[: rows - top_ref.shape[0]] = part[top_ref.shape[0] :]

    put()
    low_ref[low_ref.shape[0] - RIDE :] = squares(vector)

    @pl.when(jnp.max(number_ref[...]) > slots - early)
    def _():
        picked_ref[...] = pick_pieces(pick_ref[:early], vector_ref[...])
        for piece, blocks_ref in enumerate(blocks_refs[: pl.cdiv(early, share)]):

            @pl.loop(0, min(share, early - piece * share) // GROUP)
            def _(group):
                at = pl.multiple_of(group * GROUP, GROUP)
                here = pl.ds(pl.multiple_of(piece * share + at, GROUP), GROUP)
                prod_ref[here] = group_products(picked_ref[here], blocks_ref[pl.ds(at, GROUP)])

        put()


def end_kernel(top_in_ref, low_in_ref, before_ref, before_norm_ref, square_ref, vector_ref, norm_ref):
    rows = low_in_ref.shape[0] - RIDE
    norm = norm_row(low_in_ref[rows:])
    summed = jnp.concatenate([top_in_ref[...], low_in_ref[:rows]], 0)
    vector = recur(summed, norm, (before_ref, before_norm_ref), slice(None))
    square_ref[...] = squares(vector)
    vector_ref[...] = vector
    norm_ref[...] = jnp.broadcast_to(norm, norm_ref.shape)


def update_kernel(steps, data_vector_ref, *refs):
    alphas, refs = [r[:1] for r in refs[:steps]], refs[steps:]
    betas, refs = [r[:1] for r in refs[: steps + 1]], refs[steps + 1 :]
    models, (solution_ref, search_ref, basis_ref, coef_ref) = refs[:steps], refs[steps:]
    basis_ref[...] = data_vector_ref[...] * (1.0 / betas[-1])
    search = models[0][...] * (1.0 / alphas[0])
    solution = jnp.zeros_like(search)
    phibar, rhobar = betas[0], alphas[0]
    for step in range(steps):
        rho = jnp.sqrt(rhobar * rhobar + betas[step + 1] * betas[step + 1])
        cosine, sine = rhobar / rho, betas[step + 1] / rho
        solution = solution + (cosine * phibar / rho) * search
        phibar = sine * phibar
        if step + 1 < steps:
            rhobar = -cosine * alphas[step + 1]
            search = models[step + 1][...] * (1.0 / alphas[step + 1]) - (sine * alphas[step + 1] / rho) * search
    solution_ref[...] = solution
    search_ref[...] = search
    coef_ref[...] = jnp.broadcast_to(sine / rho, coef_ref.shape)


def search_kernel(square_ref, vector_ref, search_ref, coef_ref, out_ref):
    alpha = norm_row(square_ref[...])
    out_ref[...] = vector_ref[...] * (1.0 / alpha) - (coef_ref[:1] * alpha) * search_ref[...]


VMEM = pl.BlockSpec(memory_space=pltpu.VMEM)


def call(kernel, outs, args, scratch=(), specs=None):
    return pl.pallas_call(
        kernel,
        out_shape=[jax.ShapeDtypeStruct(o, jnp.float32) if isinstance(o, tuple) else o for o in outs],
        in_specs=specs or [VMEM] * len(args),
        out_specs=[VMEM] * len(outs),
        scratch_shapes=list(scratch),
        cost_estimate=pl.CostEstimate(flops=2 * 10**9, bytes_accessed=2**20, transcendentals=0),
        compiler_params=pltpu.CompilerParams(vmem_limit_bytes=VMEM_LIMIT),
    )(*args)


def all_sum(chunks, orders, turns, axis, size):
    chunks = list(chunks)
    stages = len(orders[0])
    for stage in range(stages):
        for at in turns:
            pairs = [(i, i ^ orders[at][stage]) for i in range(size)]
            other = lax.ppermute(chunks[at], axis, pairs)
            chunks[at] = chunks[at] + other
    return chunks


def per_device(n_row, n_col, blocks, block_rows, block_cols, counts, data):
    tile_blocks = blocks[0, 0]
    slots, _, width = tile_blocks.shape
    data = data.reshape(-1, width)
    tile_rows, tile_cols = data.shape[0], TILE_COLS
    row_bits = [1 << k for k in range(n_row.bit_length() - 1)]
    col_bits = [1 << k for k in range(n_col.bit_length() - 1)]
    row_orders, col_orders = [row_bits, row_bits], [col_bits[::-1], col_bits]
    tile, model, basis = (RIDE, width), (tile_cols, width), (tile_rows, width)

    def chunks(rows):
        return [(rows // 2, width), (rows - rows // 2 + RIDE, width)]

    def coded(*shape):
        return jax.ShapeDtypeStruct(shape, jnp.bfloat16)

    products = pltpu.VMEM((slots, width), jnp.float32)
    hbm, smem = pl.BlockSpec(memory_space=pltpu.HBM), pl.BlockSpec(memory_space=pltpu.SMEM)
    inputs = [
        pltpu.with_memory_space_constraint(a, pltpu.HBM) for a in (block_rows[0], block_cols[0], data, tile_blocks)
    ]
    *parts, data, pick_row, put_row, pick_col, put_col, order, number_f, number_a, tile_blocks = call(
        first_kernel,
        [
            *chunks(tile_cols), basis, coded(slots, tile_rows), coded(tile_rows, slots),
            coded(slots, tile_cols), coded(tile_cols, slots),
            *[jax.ShapeDtypeStruct(shape, jnp.int32) for shape in ((2, slots), tile, tile)], coded(*tile_blocks.shape),
        ],
        [inputs[0], inputs[1], counts, inputs[2], inputs[3]],
        [
            products, pltpu.VMEM((1, slots), jnp.int32), pltpu.VMEM((1, slots), jnp.int32),
            pltpu.SemaphoreType.DMA((3,)), pltpu.SemaphoreType.DMA((len(LOADS),)),
        ],
        [hbm, hbm, smem, hbm, hbm],
    )
    share = slots // PIECES
    plain, flipped = [], []
    for at in range(PIECES):
        pieces = call(
            functools.partial(arrange_kernel, at * share),
            [coded(share, width, width)] * 2,
            [order, tile_blocks],
            specs=[smem, VMEM],
        )
        plain.append(pieces[0])
        flipped.append(pieces[1])
    early = (slots // GROUP // 2 - 1) * GROUP

    def product(number, pick, put, parts, orders, axis, size, stacks, previous, out_rows, vector_rows):
        top, low = all_sum(parts, orders, TURNS[axis], axis, size)
        low_rows = low.shape[0] - RIDE
        low_vector, norm, done = call(
            functools.partial(early_kernel, PIECES),
            [(low_rows, width), tile, (early, width)],
            [pick, low, *stacks, *previous],
        )
        *parts, vector = call(
            functools.partial(rest_kernel, PIECES),
            [*chunks(out_rows), (vector_rows, width)],
            [number, pick, put, top, low_vector, norm, done, *stacks, *previous],
            [pltpu.VMEM((early, width), jnp.bfloat16), products],
        )
        return parts, vector, norm

    alphas, betas, models = [], [], []
    bases = [data]
    for _ in range(ITERS):
        previous = [models[-1], alphas[-1]] if models else []
        parts, vector, beta = product(
            number_f, pick_col, put_row, parts, row_orders, "row", n_row, flipped, previous, tile_rows, tile_cols
        )
        models.append(vector)
        betas.append(beta)
        parts, vector, alpha = product(
            number_a, pick_row, put_col, parts, col_orders, "col", n_col, plain,
            [bases[-1], beta], tile_cols, tile_rows,
        )
        bases.append(vector)
        alphas.append(alpha)
    summed = all_sum(parts, row_orders, TURNS["row"], "row", n_row)
    square, vector, beta = call(end_kernel, [tile, model, tile], [*summed, models[-1], alphas[-1]])
    solution, search, data_basis, coef = call(
        functools.partial(update_kernel, ITERS),
        [model, model, basis, tile],
        [bases[-1], *alphas, *betas, beta, *models],
    )
    (square,) = all_sum([square], [col_bits], [0], "col", n_col)
    (search,) = call(search_kernel, [model], [square, vector, search, coef])
    return solution.reshape(-1), search.reshape(-1), data_basis.reshape(-1)


def solution(mesh):
    in_specs = (
        P("row", "col", None, None, None),
        P("row", "col", None),
        P("row", "col", None),
        P("row", "col"),
        P("row"),
    )
    out_specs = (P("col"), P("col"), P("row"))
    return jax.shard_map(
        functools.partial(per_device, mesh.shape["row"], mesh.shape["col"]),
        mesh=mesh,
        in_specs=in_specs,
        out_specs=out_specs,
        check_vma=False,
    )
```

```python
import functools

import jax
import jax.numpy as jnp
from jax import lax
from jax.experimental import pallas as pl
from jax.experimental.pallas import tpu as pltpu
from jax.sharding import PartitionSpec as P


TILE_COLS = 256
ITERS = 3
EPS = 1e-06
VMEM_LIMIT = 4 * 1024 * 1024
GROUP = 16
PIECES = 2
LOADS = (9, 6, 1)
AHEAD = 2
TURNS = {"row": (1, 0), "col": (1, 0)}
RIDE = 8


def halves(values):
    high = values.astype(jnp.bfloat16)
    low = (values - high.astype(jnp.float32)).astype(jnp.bfloat16)
    return jnp.concatenate([high, low], 0)


def squares(vector):
    rows, width = vector.shape
    return jnp.sum((vector * vector).reshape(rows // RIDE, RIDE, width), 0)


def norm_row(tile):
    total = jnp.sum(jnp.sum(tile, 0, keepdims=True), 1, keepdims=True)
    return jnp.broadcast_to(jnp.sqrt(total + EPS), (1, tile.shape[1]))


def pick_pieces(pick, vector):
    return jnp.dot(
        pick, vector.astype(jnp.bfloat16), preferred_element_type=jnp.float32
    ).astype(jnp.bfloat16)


def group_products(picked, stack):
    group, width = picked.shape
    shape = (group, group * width)
    mine = lax.broadcasted_iota(jnp.int32, shape, 1) // width == lax.broadcasted_iota(jnp.int32, shape, 0)
    spread = jnp.where(mine, jnp.concatenate([picked] * group, 1), jnp.bfloat16(0))
    return jnp.dot(spread, stack.reshape(group * width, width), preferred_element_type=jnp.float32)


def put_products(put, products):
    return jnp.dot(
        jnp.concatenate([put, put], 1), halves(products), preferred_element_type=jnp.float32
    )


def first_kernel(
    rows_hbm, cols_hbm, count_ref, data_hbm, blocks_hbm,
    top_ref, low_ref, data_ref, pick_row_ref, put_row_ref, pick_col_ref, put_col_ref, order_ref, number_f_ref, number_a_ref, blocks_ref,
    prod_ref, rows_ref, cols_ref, small_sems, block_sems,
):
    slots = blocks_ref.shape[0]
    starts = [slots * sum(LOADS[:part]) // sum(LOADS) for part in range(len(LOADS))]
    small = []
    for at, pair in enumerate(((rows_hbm, rows_ref), (cols_hbm, cols_ref), (data_hbm, data_ref))):
        small.append(pltpu.make_async_copy(*pair, small_sems.at[at]))
        small[-1].start()
    copies = []
    for part, start in enumerate(starts):
        piece = pl.ds(start, slots * LOADS[part] // sum(LOADS))
        copies.append(pltpu.make_async_copy(blocks_hbm.at[piece], blocks_ref.at[piece], block_sems.at[part]))
    for copy in copies[:AHEAD]:
        copy.start()
    square = (slots, slots)
    slot = lax.broadcasted_iota(jnp.int32, (1, slots), 1)
    down = lax.broadcasted_iota(jnp.int32, square, 0)
    live = slot < count_ref[0, 0]

    def one_hot(index_ref, size):
        places = lax.broadcasted_iota(jnp.int32, (size, slots), 0)
        put = jnp.where((places == index_ref[...]) & live, 1.0, 0.0)
        return put.T.astype(jnp.bfloat16), put.astype(jnp.bfloat16)

    def ordered(index_ref, size):
        late = index_ref[...] < size // 2
        key = (jnp.where(live, jnp.where(late, 2, 0), 1) * slots + slot).astype(jnp.float32)
        keys = jnp.broadcast_to(key, square)
        place = jnp.sum(jnp.where(keys.T < keys, 1.0, 0.0), 0, keepdims=True).astype(jnp.int32)
        moved = jnp.where(down == place, 1.0, 0.0).astype(jnp.bfloat16)
        ids = jnp.broadcast_to(slot, (RIDE, slots)).astype(jnp.float32).astype(jnp.bfloat16)
        order = lax.dot_general(ids, moved, (((1,), (1,)), ((), ())), preferred_element_type=jnp.float32)
        number = jnp.sum(jnp.where(live & late, 1.0, 0.0), 1, keepdims=True)
        return moved, order[:1].astype(jnp.int32), jnp.broadcast_to(number, number_f_ref.shape).astype(jnp.int32)

    for copy in small[:2]:
        copy.wait()
    sizes = data_ref.shape[0], put_col_ref.shape[0]
    pick_row, put_row = one_hot(rows_ref, sizes[0])
    pick_col, put_col = one_hot(cols_ref, sizes[1])
    moved_f, order_ref[:1], number_f_ref[...] = ordered(cols_ref, sizes[1])
    moved_a, order_ref[1:], number_a_ref[...] = ordered(rows_ref, sizes[0])
    for moved, pick, put, to_pick_ref, to_put_ref in (
        (moved_f, pick_col, put_row, pick_col_ref, put_row_ref),
        (moved_a, pick_row, put_col, pick_row_ref, put_col_ref),
    ):
        to_pick_ref[...] = jnp.dot(moved, pick, preferred_element_type=jnp.float32).astype(jnp.bfloat16)
        to_put_ref[...] = lax.dot_general(
            put, moved, (((1,), (1,)), ((), ())), preferred_element_type=jnp.float32
        ).astype(jnp.bfloat16)
    small[2].wait()
    vector = data_ref[...]
    picked = pick_pieces(pick_row, vector)
    for at in range(0, slots, GROUP):
        if at in starts:
            part = starts.index(at)
            copies[part].wait()
            for copy in copies[part + AHEAD : part + AHEAD + 1]:
                copy.start()
        here = slice(at, at + GROUP)
        prod_ref[here] = group_products(picked[here], blocks_ref[here])
    part = put_products(put_col, prod_ref[...])
    rows, top = part.shape[0], top_ref.shape[0]
    top_ref[...] = part[:top]
    low_ref[: rows - top] = part[top:]
    low_ref[rows - top :] = squares(vector)


def arrange_kernel(first, order_ref, blocks_ref, plain_ref, flipped_ref):
    for slot in range(flipped_ref.shape[0]):
        flipped_ref[slot] = blocks_ref[order_ref[0, first + slot]].T
        plain_ref[slot] = blocks_ref[order_ref[1, first + slot]]


def recur(summed, norm, previous, here):
    vector = summed * (1.0 / norm)
    if previous:
        before_ref, before_norm_ref = previous
        vector = vector - (norm / before_norm_ref[:1]) * before_ref[here]
    return vector


def stack_of(blocks_refs, at):
    share = blocks_refs[0].shape[0]
    return blocks_refs[at // share][at % share : at % share + GROUP]


def early_kernel(pieces, pick_ref, low_in_ref, *refs):
    blocks_refs, refs = refs[:pieces], refs[pieces:]
    *previous, vector_ref, norm_ref, early_ref = refs
    rows, early = vector_ref.shape[0], early_ref.shape[0]
    norm = norm_row(low_in_ref[rows:])
    norm_ref[...] = jnp.broadcast_to(norm, norm_ref.shape)
    size = pick_ref.shape[1]
    vector = recur(low_in_ref[:rows], norm, previous, slice(size - rows, size))
    vector_ref[...] = vector
    picked = pick_pieces(pick_ref[:early, size - rows :], vector)
    for at in range(0, early, GROUP):
        early_ref[at : at + GROUP] = group_products(picked[at : at + GROUP], stack_of(blocks_refs, at))


def rest_kernel(pieces, number_ref, pick_ref, put_ref, top_in_ref, low_vector_ref, norm_ref, early_ref, *refs):
    blocks_refs, refs = refs[:pieces], refs[pieces:]
    *previous, top_ref, low_ref, vector_ref, picked_ref, prod_ref = refs
    top = top_in_ref.shape[0]
    vector = jnp.concatenate(
        [recur(top_in_ref[...], norm_ref[:1], previous, slice(0, top)), low_vector_ref[...]], 0
    )
    vector_ref[...] = vector
    slots, early, share = pick_ref.shape[0], early_ref.shape[0], blocks_refs[0].shape[0]
    picked = pick_pieces(pick_ref[early:], vector)
    prod_ref[:early] = early_ref[...]
    for at in range(early, slots, GROUP):
        here = slice(at - early, at - early + GROUP)
        prod_ref[at : at + GROUP] = group_products(picked[here], stack_of(blocks_refs, at))

    def put():
        part = put_products(put_ref[...], prod_ref[...])
        rows = part.shape[0]
        top_ref[...] = part[: top_ref.shape[0]]
        low_ref[: rows - top_ref.shape[0]] = part[top_ref.shape[0] :]

    put()
    low_ref[low_ref.shape[0] - RIDE :] = squares(vector)

    @pl.when(jnp.max(number_ref[...]) > slots - early)
    def _():
        picked_ref[...] = pick_pieces(pick_ref[:early], vector_ref[...])
        for piece, blocks_ref in enumerate(blocks_refs[: pl.cdiv(early, share)]):

            @pl.loop(0, min(share, early - piece * share) // GROUP)
            def _(group):
                at = pl.multiple_of(group * GROUP, GROUP)
                here = pl.ds(pl.multiple_of(piece * share + at, GROUP), GROUP)
                prod_ref[here] = group_products(picked_ref[here], blocks_ref[pl.ds(at, GROUP)])

        put()


def end_kernel(top_in_ref, low_in_ref, before_ref, before_norm_ref, square_ref, vector_ref, norm_ref):
    rows = low_in_ref.shape[0] - RIDE
    norm = norm_row(low_in_ref[rows:])
    summed = jnp.concatenate([top_in_ref[...], low_in_ref[:rows]], 0)
    vector = recur(summed, norm, (before_ref, before_norm_ref), slice(None))
    square_ref[...] = squares(vector)
    vector_ref[...] = vector
    norm_ref[...] = jnp.broadcast_to(norm, norm_ref.shape)


def update_kernel(steps, data_vector_ref, *refs):
    alphas, refs = [r[:1] for r in refs[:steps]], refs[steps:]
    betas, refs = [r[:1] for r in refs[: steps + 1]], refs[steps + 1 :]
    models, (solution_ref, search_ref, basis_ref, coef_ref) = refs[:steps], refs[steps:]
    basis_ref[...] = data_vector_ref[...] * (1.0 / betas[-1])
    search = models[0][...] * (1.0 / alphas[0])
    solution = jnp.zeros_like(search)
    phibar, rhobar = betas[0], alphas[0]
    for step in range(steps):
        rho = jnp.sqrt(rhobar * rhobar + betas[step + 1] * betas[step + 1])
        cosine, sine = rhobar / rho, betas[step + 1] / rho
        solution = solution + (cosine * phibar / rho) * search
        phibar = sine * phibar
        if step + 1 < steps:
            rhobar = -cosine * alphas[step + 1]
            search = models[step + 1][...] * (1.0 / alphas[step + 1]) - (sine * alphas[step + 1] / rho) * search
    solution_ref[...] = solution
    search_ref[...] = search
    coef_ref[...] = jnp.broadcast_to(sine / rho, coef_ref.shape)


def search_kernel(square_ref, vector_ref, search_ref, coef_ref, out_ref):
    alpha = norm_row(square_ref[...])
    out_ref[...] = vector_ref[...] * (1.0 / alpha) - (coef_ref[:1] * alpha) * search_ref[...]


VMEM = pl.BlockSpec(memory_space=pltpu.VMEM)


def call(kernel, outs, args, scratch=(), specs=None):
    return pl.pallas_call(
        kernel,
        out_shape=[jax.ShapeDtypeStruct(o, jnp.float32) if isinstance(o, tuple) else o for o in outs],
        in_specs=specs or [VMEM] * len(args),
        out_specs=[VMEM] * len(outs),
        scratch_shapes=list(scratch),
        cost_estimate=pl.CostEstimate(flops=2 * 10**9, bytes_accessed=2**20, transcendentals=0),
        compiler_params=pltpu.CompilerParams(vmem_limit_bytes=VMEM_LIMIT),
    )(*args)


def all_sum(chunks, orders, turns, axis, size):
    chunks = list(chunks)
    stages = len(orders[0])
    for stage in range(stages):
        for at in turns:
            pairs = [(i, i ^ orders[at][stage]) for i in range(size)]
            other = lax.ppermute(chunks[at], axis, pairs)
            chunks[at] = chunks[at] + other
    return chunks


def per_device(n_row, n_col, blocks, block_rows, block_cols, counts, data):
    tile_blocks = blocks[0, 0]
    slots, _, width = tile_blocks.shape
    data = data.reshape(-1, width)
    tile_rows, tile_cols = data.shape[0], TILE_COLS
    row_bits = [1 << k for k in range(n_row.bit_length() - 1)]
    col_bits = [1 << k for k in range(n_col.bit_length() - 1)]
    row_orders, col_orders = [row_bits, row_bits], [col_bits[::-1], col_bits]
    tile, model, basis = (RIDE, width), (tile_cols, width), (tile_rows, width)

    def chunks(rows):
        return [(rows // 2, width), (rows - rows // 2 + RIDE, width)]

    def coded(*shape):
        return jax.ShapeDtypeStruct(shape, jnp.bfloat16)

    products = pltpu.VMEM((slots, width), jnp.float32)
    hbm, smem = pl.BlockSpec(memory_space=pltpu.HBM), pl.BlockSpec(memory_space=pltpu.SMEM)
    inputs = [
        pltpu.with_memory_space_constraint(a, pltpu.HBM) for a in (block_rows[0], block_cols[0], data, tile_blocks)
    ]
    *parts, data, pick_row, put_row, pick_col, put_col, order, number_f, number_a, tile_blocks = call(
        first_kernel,
        [
            *chunks(tile_cols), basis, coded(slots, tile_rows), coded(tile_rows, slots),
            coded(slots, tile_cols), coded(tile_cols, slots),
            *[jax.ShapeDtypeStruct(shape, jnp.int32) for shape in ((2, slots), tile, tile)], coded(*tile_blocks.shape),
        ],
        [inputs[0], inputs[1], counts, inputs[2], inputs[3]],
        [
            products, pltpu.VMEM((1, slots), jnp.int32), pltpu.VMEM((1, slots), jnp.int32),
            pltpu.SemaphoreType.DMA((3,)), pltpu.SemaphoreType.DMA((len(LOADS),)),
        ],
        [hbm, hbm, smem, hbm, hbm],
    )
    share = slots // PIECES
    plain, flipped = [], []
    for at in range(PIECES):
        pieces = call(
            functools.partial(arrange_kernel, at * share),
            [coded(share, width, width)] * 2,
            [order, tile_blocks],
            specs=[smem, VMEM],
        )
        plain.append(pieces[0])
        flipped.append(pieces[1])
    early = (slots // GROUP // 2 - 1) * GROUP

    def product(number, pick, put, parts, orders, axis, size, stacks, previous, out_rows, vector_rows):
        top, low = all_sum(parts, orders, TURNS[axis], axis, size)
        low_rows = low.shape[0] - RIDE
        low_vector, norm, done = call(
            functools.partial(early_kernel, PIECES),
            [(low_rows, width), tile, (early, width)],
            [pick, low, *stacks, *previous],
        )
        *parts, vector = call(
            functools.partial(rest_kernel, PIECES),
            [*chunks(out_rows), (vector_rows, width)],
            [number, pick, put, top, low_vector, norm, done, *stacks, *previous],
            [pltpu.VMEM((early, width), jnp.bfloat16), products],
        )
        return parts, vector, norm

    alphas, betas, models = [], [], []
    bases = [data]
    for _ in range(ITERS):
        previous = [models[-1], alphas[-1]] if models else []
        parts, vector, beta = product(
            number_f, pick_col, put_row, parts, row_orders, "row", n_row, flipped, previous, tile_rows, tile_cols
        )
        models.append(vector)
        betas.append(beta)
        parts, vector, alpha = product(
            number_a, pick_row, put_col, parts, col_orders, "col", n_col, plain,
            [bases[-1], beta], tile_cols, tile_rows,
        )
        bases.append(vector)
        alphas.append(alpha)
    summed = all_sum(parts, row_orders, TURNS["row"], "row", n_row)
    square, vector, beta = call(end_kernel, [tile, model, tile], [*summed, models[-1], alphas[-1]])
    solution, search, data_basis, coef = call(
        functools.partial(update_kernel, ITERS),
        [model, model, basis, tile],
        [bases[-1], *alphas, *betas, beta, *models],
    )
    (square,) = all_sum([square], [col_bits], [0], "col", n_col)
    (search,) = call(search_kernel, [model], [square, vector, search, coef])
    return solution.reshape(-1), search.reshape(-1), data_basis.reshape(-1)


def solution(mesh):
    in_specs = (
        P("row", "col", None, None, None),
        P("row", "col", None),
        P("row", "col", None),
        P("row", "col"),
        P("row"),
    )
    out_specs = (P("col"), P("col"), P("row"))
    return jax.shard_map(
        functools.partial(per_device, mesh.shape["row"], mesh.shape["col"]),
        mesh=mesh,
        in_specs=in_specs,
        out_specs=out_specs,
        check_vma=False,
    )
```
